256 devices in a mesh: pb: 64 (over z, y_hi, x), br: 4 (over y_lo, core).
Axes of the slice: x: 4, y: 4 (y_hi: 2, y_lo: 2; y = y_hi * 2 + y_lo), z: 8, core: 2. Of those that a mesh axis runs over, the one named last changes fastest.
Arguments:
- bloch_const: bfloat16 [36, 663552], P(None, 'pb'), may hold values from -1 to 1
- polarization: bfloat16 [36, 512, 36], P('br', 'pb'), may hold values from -1 to 1
- delta_weight: bfloat16 [36, 512, 18432], P('br', None, 'pb'), may hold values from 0.02 to 3
- partner: int32 [512, 512], P('pb'), may hold values from 0 to 511, each once within a row
- velocity: float32 [512, 36], P('pb', 'br'), may hold values from -0.5 to 1.5
- capacity: float32 [512, 36], P('pb', 'br'), may hold values from 0.2 to 2
Outputs:
- deviation: float32 [512, 36], P('pb', 'br')
- kappa: float32 [2], replicated
The draws below stay inside these ranges and needn't reach their ends.
Inputs may be any that keep to these rules, and one draw needn't show every extreme that they name: For each q, partner[q, :] names every q-point exactly once.
All inputs are finite; a program needn't handle non-finite values.
Results may differ from the reference program's by a relative error of at most 0.0003.
Values may be sent and summed in bfloat16 or wider, within the bound.
A program may use at most 192 MiB of HBM per device.

```python
import math
import jax
import jax.numpy as jnp
from jax import lax

NB = 36
M = 36
Q_DEV = 8
ITERS = 2
NQ = 512


def draw_delta_weight(key, part):
    block_count = NQ // Q_DEV
    target_point = lax_free_iota((1, NQ, 1), 1)
    column = lax_free_iota((1, 1, NQ * NB), 2)
    source_point = column // NB
    heavy = target_point // Q_DEV == (source_point // Q_DEV + block_count // 2) % block_count
    spread = jax.random.uniform(key, (NB, NQ, NQ * NB), jnp.float32)
    light_value = 0.02 * jnp.exp(spread * math.log(5.0))
    heavy_value = 1.5 * jnp.exp(spread * math.log(2.0))
    return jnp.where(heavy, heavy_value, light_value).astype(jnp.bfloat16)


def lax_free_iota(shape, axis):
    return jnp.broadcast_to(jnp.arange(shape[axis], dtype=jnp.int32).reshape([shape[i] if i == axis else 1 for i in range(len(shape))]), shape)


def draw_velocity(key, part):
    key_phase, key_noise = jax.random.split(jax.random.fold_in(key, 17))
    phase = jax.random.uniform(key_phase, (), jnp.float32, -math.pi, math.pi)
    point = lax_free_iota((NQ, NB), 0)
    branch = lax_free_iota((NQ, NB), 1)
    block_center = ((point // Q_DEV).astype(jnp.float32) + 0.5) * (Q_DEV / NQ)
    wave = jnp.sin(2.0 * math.pi * block_center + phase)
    amplitude = jnp.where(branch % 2 == 0, 0.7, 0.5)
    noise = jnp.clip(0.15 * jax.random.normal(key_noise, (NQ, NB), jnp.float32), -0.3, 0.3)
    return 0.5 + amplitude * wave + noise


def block_scale(own_key, extent, pieces, smallest, top_value):
    loudness = 1.0
    for dim, shards_of in pieces:
        steps = jax.random.uniform(jax.random.fold_in(jax.random.fold_in(own_key, 6), dim), (shards_of,), jnp.float32, smallest / len(pieces), top_value / len(pieces))
        loudness = loudness * jnp.repeat(jnp.exp(steps), extent[dim] // shards_of).reshape((-1,) + (1,) * (len(extent) - 1 - dim))
    return loudness


def bell_draw(rng, extent, width, bound, pieces=(), kind=jnp.bfloat16):
    level = block_scale(rng, extent, pieces, -0.22, 0.18) if pieces else 1.0
    values = jax.random.normal(rng, extent, jnp.float32) * width * level
    return jnp.minimum(jnp.maximum(values, -bound), bound).astype(kind)


def setup_inputs(seed: int = 0) -> dict:
    arg_keys = jax.random.split(jax.random.key(seed), 7)
    bloch_const = bell_draw(arg_keys[0], (M, NQ * NB * M), M ** -0.5, 1.0, ((1, 64),))
    polarization = bell_draw(arg_keys[1], (NB, NQ, M), M ** -0.5, 1.0, ((0, 4), (1, 64)))
    delta_weight = draw_delta_weight(jax.random.fold_in(arg_keys[6], 71), 0)
    partner = jax.vmap(lambda own: jax.random.permutation(own, NQ))(jax.random.split(arg_keys[3], NQ)).reshape((NQ, NQ)).astype(jnp.int32)
    velocity = draw_velocity(jax.random.fold_in(arg_keys[6], 71), 0)
    capacity = jnp.clip(jnp.exp(math.log(2.0) - 2.3025851 * jax.random.uniform(arg_keys[5], (NQ, NB), jnp.float32) ** block_scale(arg_keys[5], (NQ, NB), ((0, 64), (1, 4)), -0.2, 0.2)), 0.2, 2.0)
    return {"bloch_const": bloch_const, "polarization": polarization, "delta_weight": delta_weight, "partner": partner, "velocity": velocity, "capacity": capacity}


def reference(bloch_const, polarization, delta_weight, partner, velocity, capacity):
    polar_rows = polarization.astype(jnp.float32).reshape(NB * NQ, M)
    inv_count = 1.0 / (NQ * NB)

    def per_point(point):
        const_block = lax.dynamic_slice_in_dim(bloch_const, point * (NB * M), NB * M, 1).astype(jnp.float32)
        amplitude = jnp.dot(polar_rows, const_block, precision=lax.Precision.HIGHEST).reshape(NB * NQ, NB, M)
        squared = jnp.sum(amplitude * amplitude, axis=2)
        weight_block = lax.dynamic_slice_in_dim(delta_weight, point * NB, NB, 2).astype(jnp.float32).reshape(NB * NQ, NB)
        return squared * weight_block * inv_count

    coupling = lax.map(per_point, jnp.arange(NQ, dtype=jnp.int32))
    rate_total = jnp.sum(coupling, axis=1)
    deviation = velocity / rate_total
    kappas = []
    for sweep_index in range(ITERS):
        flattened = jnp.transpose(deviation).reshape(NB * NQ)
        partner_value = jnp.transpose(deviation[partner], (0, 2, 1)).reshape(NQ, NB * NQ)
        combined = flattened[None, :] + partner_value
        spread = jnp.einsum("qas,qa->qs", coupling, combined, precision=lax.Precision.HIGHEST)
        deviation = (velocity + 0.5 * spread) / rate_total
        kappas.append(jnp.sum(capacity * velocity * deviation) * inv_count)
    return deviation, jnp.stack(kappas)
```

```python
from functools import partial

import jax
import jax.numpy as jnp
from jax import lax
from jax.sharding import PartitionSpec as P

ITERS = 2


def split_points(bloch_const, local_points, chosen):
    components = bloch_const.shape[0]
    reshaped = bloch_const.reshape(components, local_points, -1, components)
    return jnp.transpose(reshaped.reshape(components, local_points, chosen * components), (1, 0, 2))


def coupling_fold(carried, shard_in, first_row, const_blocks, delta_local, inv_count):
    lead_size = shard_in.shape[0]
    piece_len = shard_in.shape[1]
    components = shard_in.shape[2]
    flat_rows = shard_in.reshape(lead_size * piece_len, components)

    def per_point(const_block):
        amplitude = jnp.dot(flat_rows, const_block, preferred_element_type=jnp.float32)
        amplitude = amplitude.reshape(lead_size * piece_len, -1, components)
        return jnp.sum(amplitude * amplitude, axis=2)

    squared = lax.map(per_point, const_blocks)
    squared = jnp.transpose(squared, (1, 0, 2)).reshape(lead_size, piece_len, -1)
    weight_block = delta_local.astype(jnp.float32)
    return squared * weight_block * inv_count


def branch_total(partial_sum):
    own_count = partial_sum.shape[1] // lax.axis_size("br")
    summed = lax.psum(partial_sum, "br")
    return lax.dynamic_slice_in_dim(summed, lax.axis_index("br") * own_count, own_count, 1)


def gather_pb(block, axis):
    count = lax.axis_size("pb")
    copies = jnp.broadcast_to(block[None], (count,) + block.shape)
    got = lax.all_to_all(copies, "pb", 0, 0, tiled=True)
    got = jnp.moveaxis(got, 0, axis)
    shape = list(block.shape)
    shape[axis] *= count
    return got.reshape(shape)


def full_deviation(deviation):
    return gather_pb(deviation, 0)


def on_device(bloch_const, polarization, delta_weight, partner, velocity, capacity):
    local_points = velocity.shape[0]
    own_count = velocity.shape[1]
    all_branches = own_count * lax.axis_size("br")
    total_points = polarization.shape[1] * lax.axis_size("pb")
    inv_count = 1.0 / (total_points * all_branches)
    const_blocks = split_points(bloch_const, local_points, all_branches)
    zero_start = jnp.zeros((own_count, total_points, local_points * all_branches), jnp.float32)
    folder = partial(
        coupling_fold, const_blocks=const_blocks, delta_local=delta_weight, inv_count=inv_count
    )
    coupling = folder(zero_start, gather_pb(polarization, 1), jnp.int32(0))
    coupling = coupling.reshape(own_count, total_points, local_points, all_branches)
    rate_total = branch_total(jnp.sum(coupling, axis=(0, 1)))
    deviation = velocity / rate_total
    heat_weight = capacity * velocity
    kappas = []
    for sweep_index in range(ITERS):
        deviation_all = full_deviation(deviation)
        partner_value = deviation_all[partner]
        combined = jnp.transpose(deviation_all)[:, :, None] + jnp.transpose(
            partner_value, (2, 1, 0)
        )
        spread = jnp.einsum("abqs,abq->qs", coupling, combined, precision=lax.Precision.HIGHEST)
        spread = branch_total(spread)
        deviation = (velocity + 0.5 * spread) / rate_total
        kappas.append(jnp.sum(heat_weight * deviation))
    axes = ("pb", "br")
    devices = lax.axis_size(axes)
    partials = jnp.broadcast_to(jnp.stack(kappas)[None], (devices, ITERS))
    kappa = jnp.sum(lax.all_to_all(partials, axes, 0, 0, tiled=True), axis=0) * inv_count
    return (deviation, kappa)


def solution(mesh):
    in_specs = (
        P(None, "pb"),
        P("br", "pb", None),
        P("br", None, "pb"),
        P("pb", None),
        P("pb", "br"),
        P("pb", "br"),
    )
    out_specs = (P("pb", "br"), P())
    return jax.shard_map(
        on_device, mesh=mesh, in_specs=in_specs, out_specs=out_specs, check_vma=False
    )
```

```python
from functools import partial

import jax
import jax.numpy as jnp
from jax import lax
from jax.experimental import pallas as pl
from jax.experimental.pallas import tpu as pltpu
from jax.sharding import PartitionSpec as P

ITERS = 2


def coupling_kernel(bt_ref, pt_ref, dw_ref, out_ref, acc_ref, *, inv_count):
    pt = pt_ref[...]
    acc_ref[...] = jnp.zeros(acc_ref.shape, jnp.float32)

    def body(n, carry):
        amp = jnp.dot(bt_ref[n], pt, preferred_element_type=jnp.float32)
        acc_ref[...] += amp * amp
        return carry

    lax.fori_loop(0, bt_ref.shape[0], body, 0)
    out_ref[...] = acc_ref[...] * dw_ref[...].astype(jnp.float32) * inv_count


def coupling_call(bt, pt, dw, inv_count, tile=512):
    comps, rows, m = bt.shape
    cols = pt.shape[1]
    return pl.pallas_call(
        partial(coupling_kernel, inv_count=inv_count),
        grid=(cols // tile,),
        in_specs=[
            pl.BlockSpec((comps, rows, m), lambda i: (0, 0, 0)),
            pl.BlockSpec((m, tile), lambda i: (0, i)),
            pl.BlockSpec((rows, tile), lambda i: (0, i)),
        ],
        out_specs=pl.BlockSpec((rows, tile), lambda i: (0, i)),
        out_shape=jax.ShapeDtypeStruct((rows, cols), jnp.float32),
        scratch_shapes=[pltpu.VMEM((rows, tile), jnp.float32)],
    )(bt, pt, dw)


def branch_total(partial_sum):
    own_count = partial_sum.shape[1] // lax.axis_size("br")
    summed = lax.psum(partial_sum, "br")
    return lax.dynamic_slice_in_dim(summed, lax.axis_index("br") * own_count, own_count, 1)


def gather_pb(block, axis):
    count = lax.axis_size("pb")
    copies = jnp.broadcast_to(block[None], (count,) + block.shape)
    got = lax.all_to_all(copies, "pb", 0, 0, tiled=True)
    got = jnp.moveaxis(got, 0, axis)
    shape = list(block.shape)
    shape[axis] *= count
    return got.reshape(shape)


def full_deviation(deviation):
    return gather_pb(deviation, 0)


def on_device(bloch_const, polarization, delta_weight, partner, velocity, capacity):
    local_points = velocity.shape[0]
    own_count = velocity.shape[1]
    all_branches = own_count * lax.axis_size("br")
    total_points = polarization.shape[1] * lax.axis_size("pb")
    inv_count = 1.0 / (total_points * all_branches)
    components = bloch_const.shape[0]
    bt = bloch_const.reshape(components, local_points, all_branches, -1)
    bt = jnp.transpose(bt, (3, 1, 2, 0)).reshape(-1, local_points * all_branches, components)
    pol_all = gather_pb(polarization, 1)
    pt = jnp.transpose(pol_all, (2, 0, 1)).reshape(components, own_count * total_points)
    dw = jnp.transpose(delta_weight.reshape(own_count * total_points, -1))
    coupling_t = coupling_call(bt, pt, dw, inv_count)
    coupling = coupling_t.reshape(local_points, all_branches, own_count * total_points)
    rate_total = branch_total(jnp.sum(coupling, axis=2))
    deviation = velocity / rate_total
    heat_weight = capacity * velocity
    kappas = []
    for sweep_index in range(ITERS):
        deviation_all = full_deviation(deviation)
        partner_value = deviation_all[partner]
        combined = jnp.transpose(deviation_all)[None] + jnp.transpose(partner_value, (0, 2, 1))
        combined = combined.reshape(local_points, 1, -1)
        spread = jnp.sum(coupling * combined, axis=2)
        spread = branch_total(spread)
        deviation = (velocity + 0.5 * spread) / rate_total
        kappas.append(jnp.sum(heat_weight * deviation))
    axes = ("pb", "br")
    devices = lax.axis_size(axes)
    partials = jnp.broadcast_to(jnp.stack(kappas)[None], (devices, ITERS))
    kappa = jnp.sum(lax.all_to_all(partials, axes, 0, 0, tiled=True), axis=0) * inv_count
    return (deviation, kappa)


def solution(mesh):
    in_specs = (
        P(None, "pb"),
        P("br", "pb", None),
        P("br", None, "pb"),
        P("pb", None),
        P("pb", "br"),
        P("pb", "br"),
    )
    out_specs = (P("pb", "br"), P())
    return jax.shard_map(
        on_device, mesh=mesh, in_specs=in_specs, out_specs=out_specs, check_vma=False
    )
```

```python
from functools import partial

import jax
import jax.numpy as jnp
from jax import lax
from jax.experimental import pallas as pl
from jax.experimental.pallas import tpu as pltpu
from jax.sharding import PartitionSpec as P

ITERS = 2


def coupling_kernel(bt_ref, pt_ref, dw_ref, out_ref, acc_ref, *, inv_count):
    pt = pt_ref[...]
    acc_ref[...] = jnp.zeros(acc_ref.shape, jnp.float32)

    def body(n, carry):
        amp = jnp.dot(bt_ref[n], pt, preferred_element_type=jnp.float32)
        acc_ref[...] += amp * amp
        return carry

    lax.fori_loop(0, bt_ref.shape[0], body, 0, unroll=4)
    out_ref[...] = acc_ref[...] * dw_ref[...].astype(jnp.float32) * inv_count


def coupling_call(bt, pt, dw, inv_count, tile=2304):
    comps, rows, m = bt.shape
    cols = pt.shape[1]
    while cols % tile:
        tile //= 2
    return pl.pallas_call(
        partial(coupling_kernel, inv_count=inv_count),
        grid=(cols // tile,),
        in_specs=[
            pl.BlockSpec((comps, rows, m), lambda i: (0, 0, 0)),
            pl.BlockSpec((m, tile), lambda i: (0, i)),
            pl.BlockSpec((rows, tile), lambda i: (0, i)),
        ],
        out_specs=pl.BlockSpec((rows, tile), lambda i: (0, i)),
        out_shape=jax.ShapeDtypeStruct((rows, cols), jnp.float32),
        scratch_shapes=[pltpu.VMEM((rows, tile), jnp.float32)],
    )(bt, pt, dw)


def branch_total(partial_sum):
    own_count = partial_sum.shape[1] // lax.axis_size("br")
    summed = lax.psum(partial_sum, "br")
    return lax.dynamic_slice_in_dim(summed, lax.axis_index("br") * own_count, own_count, 1)


def gather_pb(block, axis):
    count = lax.axis_size("pb")
    copies = jnp.broadcast_to(block[None], (count,) + block.shape)
    got = lax.all_to_all(copies, "pb", 0, 0, tiled=True)
    got = jnp.moveaxis(got, 0, axis)
    shape = list(block.shape)
    shape[axis] *= count
    return got.reshape(shape)


def full_deviation(deviation):
    return gather_pb(deviation, 0)


def on_device(bloch_const, polarization, delta_weight, partner, velocity, capacity):
    local_points = velocity.shape[0]
    own_count = velocity.shape[1]
    all_branches = own_count * lax.axis_size("br")
    total_points = polarization.shape[1] * lax.axis_size("pb")
    inv_count = 1.0 / (total_points * all_branches)
    components = bloch_const.shape[0]
    bt = bloch_const.reshape(components, local_points, all_branches, -1)
    bt = jnp.transpose(bt, (3, 1, 2, 0)).reshape(-1, local_points * all_branches, components)
    pol_all = gather_pb(polarization, 1)
    pt = jnp.transpose(pol_all, (2, 0, 1)).reshape(components, own_count * total_points)
    dw = jnp.transpose(delta_weight.reshape(own_count * total_points, -1))
    coupling_t = coupling_call(bt, pt, dw, inv_count)
    coupling = coupling_t.reshape(local_points, all_branches, own_count * total_points)
    rate_total = branch_total(jnp.sum(coupling, axis=2))
    deviation = velocity / rate_total
    heat_weight = capacity * velocity
    kappas = []
    for sweep_index in range(ITERS):
        deviation_all = full_deviation(deviation)
        partner_value = deviation_all[partner]
        combined = jnp.transpose(deviation_all)[None] + jnp.transpose(partner_value, (0, 2, 1))
        combined = combined.reshape(local_points, 1, -1)
        spread = jnp.sum(coupling * combined, axis=2)
        spread = branch_total(spread)
        deviation = (velocity + 0.5 * spread) / rate_total
        kappas.append(jnp.sum(heat_weight * deviation))
    axes = ("pb", "br")
    devices = lax.axis_size(axes)
    partials = jnp.broadcast_to(jnp.stack(kappas)[None], (devices, ITERS))
    kappa = jnp.sum(lax.all_to_all(partials, axes, 0, 0, tiled=True), axis=0) * inv_count
    return (deviation, kappa)


def solution(mesh):
    in_specs = (
        P(None, "pb"),
        P("br", "pb", None),
        P("br", None, "pb"),
        P("pb", None),
        P("pb", "br"),
        P("pb", "br"),
    )
    out_specs = (P("pb", "br"), P())
    return jax.shard_map(
        on_device, mesh=mesh, in_specs=in_specs, out_specs=out_specs, check_vma=False
    )
```

```python
from functools import partial

import jax
import jax.numpy as jnp
from jax import lax
from jax.experimental import pallas as pl
from jax.experimental.pallas import tpu as pltpu
from jax.sharding import PartitionSpec as P

ITERS = 2


def coupling_kernel(bt_ref, pt_ref, dw_ref, out_ref, acc_ref, *, inv_count):
    pt = pt_ref[...]
    acc_ref[...] = jnp.zeros(acc_ref.shape, jnp.float32)

    def body(n, carry):
        amp = jnp.dot(bt_ref[n], pt, preferred_element_type=jnp.float32)
        acc_ref[...] += amp * amp
        return carry

    lax.fori_loop(0, bt_ref.shape[0], body, 0, unroll=4)
    out_ref[...] = acc_ref[...] * dw_ref[...].astype(jnp.float32) * inv_count


def coupling_call(bt, pt, dw, inv_count, tile=2304):
    comps, rows, m = bt.shape
    cols = pt.shape[1]
    while cols % tile:
        tile //= 2
    return pl.pallas_call(
        partial(coupling_kernel, inv_count=inv_count),
        grid=(cols // tile,),
        in_specs=[
            pl.BlockSpec((comps, rows, m), lambda i: (0, 0, 0)),
            pl.BlockSpec((m, tile), lambda i: (0, i)),
            pl.BlockSpec((rows, tile), lambda i: (0, i)),
        ],
        out_specs=pl.BlockSpec((rows, tile), lambda i: (0, i)),
        out_shape=jax.ShapeDtypeStruct((rows, cols), jnp.float32),
        scratch_shapes=[pltpu.VMEM((rows, tile), jnp.float32)],
    )(bt, pt, dw)


def branch_total(partial_sum):
    own_count = partial_sum.shape[1] // lax.axis_size("br")
    summed = lax.psum(partial_sum, "br")
    return lax.dynamic_slice_in_dim(summed, lax.axis_index("br") * own_count, own_count, 1)


def gather_pb(block, axis):
    count = lax.axis_size("pb")
    copies = jnp.broadcast_to(block[None], (count,) + block.shape)
    got = lax.all_to_all(copies, "pb", 0, 0, tiled=True)
    got = jnp.moveaxis(got, 0, axis)
    shape = list(block.shape)
    shape[axis] *= count
    return got.reshape(shape)


def full_deviation(deviation):
    return gather_pb(deviation, 0)


def on_device(bloch_const, polarization, delta_weight, partner, velocity, capacity):
    local_points = velocity.shape[0]
    own_count = velocity.shape[1]
    all_branches = own_count * lax.axis_size("br")
    total_points = polarization.shape[1] * lax.axis_size("pb")
    inv_count = 1.0 / (total_points * all_branches)
    components = bloch_const.shape[0]
    bt = bloch_const.reshape(components, local_points, all_branches, -1)
    bt = jnp.transpose(bt, (3, 1, 2, 0)).reshape(-1, local_points * all_branches, components)
    pol_all = gather_pb(polarization, 1)
    pt = jnp.transpose(pol_all, (2, 0, 1)).reshape(components, own_count * total_points)
    dw = jnp.transpose(delta_weight.reshape(own_count * total_points, -1))
    coupling_t = coupling_call(bt, pt, dw, inv_count)
    coupling = coupling_t.reshape(local_points, all_branches, own_count * total_points)
    rate_total = branch_total(jnp.sum(coupling, axis=2))
    by_point = coupling.reshape(local_points, all_branches * own_count, total_points)
    high = by_point.astype(jnp.bfloat16)
    rest = by_point - high.astype(jnp.float32)
    middle = rest.astype(jnp.bfloat16)
    low = (rest - middle.astype(jnp.float32)).astype(jnp.bfloat16)
    pieces = jnp.concatenate([high, middle, low], axis=1)
    targets = lax.broadcasted_iota(jnp.int32, (1, 1, total_points), 2)
    one_hot = (partner[:, :, None] == targets).astype(jnp.bfloat16)
    moved = jnp.einsum("qxa,qab->qxb", pieces, one_hot, preferred_element_type=jnp.float32)
    moved = moved.reshape(local_points, 3, -1, total_points)
    moved = (moved[:, 0] + moved[:, 1]) + moved[:, 2]
    folded = (by_point + moved).reshape(local_points * all_branches, -1)
    deviation = velocity / rate_total
    heat_weight = capacity * velocity
    kappas = []
    for sweep_index in range(ITERS):
        deviation_all = full_deviation(deviation)
        flat = jnp.transpose(deviation_all).reshape(1, -1)
        spread = jnp.sum(folded * flat, axis=1).reshape(local_points, all_branches)
        spread = branch_total(spread)
        deviation = (velocity + 0.5 * spread) / rate_total
        kappas.append(jnp.sum(heat_weight * deviation))
    axes = ("pb", "br")
    devices = lax.axis_size(axes)
    partials = jnp.broadcast_to(jnp.stack(kappas)[None], (devices, ITERS))
    kappa = jnp.sum(lax.all_to_all(partials, axes, 0, 0, tiled=True), axis=0) * inv_count
    return (deviation, kappa)


def solution(mesh):
    in_specs = (
        P(None, "pb"),
        P("br", "pb", None),
        P("br", None, "pb"),
        P("pb", None),
        P("pb", "br"),
        P("pb", "br"),
    )
    out_specs = (P("pb", "br"), P())
    return jax.shard_map(
        on_device, mesh=mesh, in_specs=in_specs, out_specs=out_specs, check_vma=False
    )
```

```python
from functools import partial

import jax
import jax.numpy as jnp
from jax import lax
from jax.experimental import pallas as pl
from jax.experimental.pallas import tpu as pltpu
from jax.sharding import PartitionSpec as P

ITERS = 2


def coupling_kernel(bt_ref, pt_ref, dw_ref, out_ref, acc_ref, *, inv_count):
    pt = pt_ref[...]
    acc_ref[...] = jnp.zeros(acc_ref.shape, jnp.float32)

    def body(n, carry):
        amp = jnp.dot(bt_ref[n], pt, preferred_element_type=jnp.float32)
        acc_ref[...] += amp * amp
        return carry

    lax.fori_loop(0, bt_ref.shape[0], body, 0, unroll=4)
    out_ref[...] = acc_ref[...] * dw_ref[...].astype(jnp.float32) * inv_count


def coupling_call(bt, pt, dw, inv_count, tile=2304):
    comps, rows, m = bt.shape
    cols = pt.shape[1]
    while cols % tile:
        tile //= 2
    return pl.pallas_call(
        partial(coupling_kernel, inv_count=inv_count),
        grid=(cols // tile,),
        in_specs=[
            pl.BlockSpec((comps, rows, m), lambda i: (0, 0, 0)),
            pl.BlockSpec((m, tile), lambda i: (0, i)),
            pl.BlockSpec((rows, tile), lambda i: (0, i)),
        ],
        out_specs=pl.BlockSpec((rows, tile), lambda i: (0, i)),
        out_shape=jax.ShapeDtypeStruct((rows, cols), jnp.float32),
        scratch_shapes=[pltpu.VMEM((rows, tile), jnp.float32)],
    )(bt, pt, dw)


def branch_total(partial_sum):
    own_count = partial_sum.shape[1] // lax.axis_size("br")
    summed = lax.psum(partial_sum, "br")
    return lax.dynamic_slice_in_dim(summed, lax.axis_index("br") * own_count, own_count, 1)


def gather_pb(block, axis):
    count = lax.axis_size("pb")
    copies = jnp.broadcast_to(block[None], (count,) + block.shape)
    got = lax.all_to_all(copies, "pb", 0, 0, tiled=True)
    got = jnp.moveaxis(got, 0, axis)
    shape = list(block.shape)
    shape[axis] *= count
    return got.reshape(shape)


def full_deviation(deviation):
    return gather_pb(deviation, 0)


def on_device(bloch_const, polarization, delta_weight, partner, velocity, capacity):
    local_points = velocity.shape[0]
    own_count = velocity.shape[1]
    all_branches = own_count * lax.axis_size("br")
    total_points = polarization.shape[1] * lax.axis_size("pb")
    inv_count = 1.0 / (total_points * all_branches)
    components = bloch_const.shape[0]
    bt = bloch_const.reshape(components, local_points, all_branches, -1)
    bt = jnp.transpose(bt, (3, 1, 2, 0)).reshape(-1, local_points * all_branches, components)
    pol_all = gather_pb(polarization, 1)
    pt = jnp.transpose(pol_all, (2, 0, 1)).reshape(components, own_count * total_points)
    dw = jnp.transpose(delta_weight.reshape(own_count * total_points, -1))
    coupling_t = coupling_call(bt, pt, dw, inv_count)
    coupling = coupling_t.reshape(local_points, all_branches, own_count * total_points)
    rate_total = branch_total(jnp.sum(coupling, axis=2))
    deviation = velocity / rate_total
    heat_weight = capacity * velocity
    coupling_rows = coupling.reshape(local_points * all_branches, -1)
    targets = lax.broadcasted_iota(jnp.int32, (1, 1, total_points), 2)
    one_hot = (partner[:, :, None] == targets).astype(jnp.bfloat16)
    own_point = lax.broadcasted_iota(jnp.int32, (local_points, all_branches, local_points), 0)
    diagonal = own_point == lax.broadcasted_iota(jnp.int32, own_point.shape, 2)
    kappas = []
    for sweep_index in range(ITERS):
        deviation_all = full_deviation(deviation)
        high = deviation_all.astype(jnp.bfloat16)
        rest = deviation_all - high.astype(jnp.float32)
        middle = rest.astype(jnp.bfloat16)
        low = (rest - middle.astype(jnp.float32)).astype(jnp.bfloat16)
        pieces = jnp.concatenate([high, middle, low], axis=1)
        moved = jnp.einsum("qab,bs->qas", one_hot, pieces, preferred_element_type=jnp.float32)
        moved = moved.reshape(local_points, total_points, 3, own_count)
        partner_value = (moved[:, :, 0] + moved[:, :, 1]) + moved[:, :, 2]
        combined = jnp.transpose(deviation_all)[None] + jnp.transpose(partner_value, (0, 2, 1))
        combined = combined.reshape(local_points, -1)
        every = jnp.dot(coupling_rows, combined.T, precision=lax.Precision.HIGHEST)
        every = every.reshape(local_points, all_branches, local_points)
        spread = jnp.sum(jnp.where(diagonal, every, 0.0), axis=2)
        spread = branch_total(spread)
        deviation = (velocity + 0.5 * spread) / rate_total
        kappas.append(jnp.sum(heat_weight * deviation))
    axes = ("pb", "br")
    devices = lax.axis_size(axes)
    partials = jnp.broadcast_to(jnp.stack(kappas)[None], (devices, ITERS))
    kappa = jnp.sum(lax.all_to_all(partials, axes, 0, 0, tiled=True), axis=0) * inv_count
    return (deviation, kappa)


def solution(mesh):
    in_specs = (
        P(None, "pb"),
        P("br", "pb", None),
        P("br", None, "pb"),
        P("pb", None),
        P("pb", "br"),
        P("pb", "br"),
    )
    out_specs = (P("pb", "br"), P())
    return jax.shard_map(
        on_device, mesh=mesh, in_specs=in_specs, out_specs=out_specs, check_vma=False
    )
```

```python
from functools import partial

import jax
import jax.numpy as jnp
from jax import lax
from jax.experimental import pallas as pl
from jax.experimental.pallas import tpu as pltpu
from jax.sharding import PartitionSpec as P

ITERS = 2


def split_three(value):
    high = value.astype(jnp.bfloat16)
    rest = value - high.astype(jnp.float32)
    middle = rest.astype(jnp.bfloat16)
    low = (rest - middle.astype(jnp.float32)).astype(jnp.bfloat16)
    return high, middle, low


def coupling_kernel(bt_ref, pt_ref, dw_ref, out_ref, parts_ref, acc_ref, *, inv_count):
    pt = pt_ref[...]
    acc_ref[...] = jnp.zeros(acc_ref.shape, jnp.float32)

    def body(n, carry):
        amp = jnp.dot(bt_ref[n], pt, preferred_element_type=jnp.float32)
        acc_ref[...] += amp * amp
        return carry

    lax.fori_loop(0, bt_ref.shape[0], body, 0, unroll=4)
    value = acc_ref[...] * dw_ref[...].astype(jnp.float32) * inv_count
    out_ref[...] = value
    high, middle, low = split_three(value)
    parts_ref[0] = high
    parts_ref[1] = middle
    parts_ref[2] = low


def coupling_call(bt, pt, dw, inv_count, tile=2304):
    comps, rows, m = bt.shape
    cols = pt.shape[1]
    while cols % tile:
        tile //= 2
    return pl.pallas_call(
        partial(coupling_kernel, inv_count=inv_count),
        grid=(cols // tile,),
        in_specs=[
            pl.BlockSpec((comps, rows, m), lambda i: (0, 0, 0)),
            pl.BlockSpec((m, tile), lambda i: (0, i)),
            pl.BlockSpec((rows, tile), lambda i: (0, i)),
        ],
        out_specs=[
            pl.BlockSpec((rows, tile), lambda i: (0, i)),
            pl.BlockSpec((3, rows, tile), lambda i: (0, 0, i)),
        ],
        out_shape=[
            jax.ShapeDtypeStruct((rows, cols), jnp.float32),
            jax.ShapeDtypeStruct((3, rows, cols), jnp.bfloat16),
        ],
        scratch_shapes=[pltpu.VMEM((rows, tile), jnp.float32)],
    )(bt, pt, dw)


def branch_total(partial_sum):
    own_count = partial_sum.shape[1] // lax.axis_size("br")
    summed = lax.psum(partial_sum, "br")
    return lax.dynamic_slice_in_dim(summed, lax.axis_index("br") * own_count, own_count, 1)


def gather_pb(block, axis):
    count = lax.axis_size("pb")
    copies = jnp.broadcast_to(block[None], (count,) + block.shape)
    got = lax.all_to_all(copies, "pb", 0, 0, tiled=True)
    got = jnp.moveaxis(got, 0, axis)
    shape = list(block.shape)
    shape[axis] *= count
    return got.reshape(shape)


def full_deviation(deviation):
    return gather_pb(deviation, 0)


def on_device(bloch_const, polarization, delta_weight, partner, velocity, capacity):
    local_points = velocity.shape[0]
    own_count = velocity.shape[1]
    all_branches = own_count * lax.axis_size("br")
    total_points = polarization.shape[1] * lax.axis_size("pb")
    inv_count = 1.0 / (total_points * all_branches)
    components = bloch_const.shape[0]
    bt = bloch_const.reshape(components, local_points, all_branches, -1)
    bt = jnp.transpose(bt, (3, 1, 2, 0)).reshape(-1, local_points * all_branches, components)
    pol_all = gather_pb(polarization, 1)
    pt = jnp.transpose(pol_all, (2, 0, 1)).reshape(components, own_count * total_points)
    dw = jnp.transpose(delta_weight.reshape(own_count * total_points, -1))
    coupling_t, coupling_parts = coupling_call(bt, pt, dw, inv_count)
    coupling = coupling_t.reshape(local_points, all_branches, own_count * total_points)
    rate_total = branch_total(jnp.sum(coupling, axis=2))
    deviation = velocity / rate_total
    heat_weight = capacity * velocity
    targets = lax.broadcasted_iota(jnp.int32, (1, 1, total_points), 2)
    one_hot = (partner[:, :, None] == targets).astype(jnp.bfloat16)
    own_point = lax.broadcasted_iota(jnp.int32, (local_points, all_branches, local_points), 0)
    diagonal = own_point == lax.broadcasted_iota(jnp.int32, own_point.shape, 2)
    kappas = []
    for sweep_index in range(ITERS):
        deviation_all = full_deviation(deviation)
        pieces = jnp.concatenate(split_three(deviation_all), axis=1)
        moved = jnp.einsum("qab,bs->qas", one_hot, pieces, preferred_element_type=jnp.float32)
        moved = moved.reshape(local_points, total_points, 3, own_count)
        partner_value = (moved[:, :, 0] + moved[:, :, 1]) + moved[:, :, 2]
        combined = jnp.transpose(deviation_all)[None] + jnp.transpose(partner_value, (0, 2, 1))
        combined = combined.reshape(local_points, -1)
        combined_parts = jnp.stack(split_three(combined))
        every = lax.dot_general(
            coupling_parts.reshape(-1, coupling_parts.shape[2]),
            combined_parts.reshape(-1, combined_parts.shape[2]),
            (((1,), (1,)), ((), ())),
            preferred_element_type=jnp.float32,
        )
        every = every.reshape(3, local_points, all_branches, 3, local_points)
        every = jnp.sum(every, axis=(0, 3))
        spread = jnp.sum(jnp.where(diagonal, every, 0.0), axis=2)
        spread = branch_total(spread)
        deviation = (velocity + 0.5 * spread) / rate_total
        kappas.append(jnp.sum(heat_weight * deviation))
    axes = ("pb", "br")
    devices = lax.axis_size(axes)
    partials = jnp.broadcast_to(jnp.stack(kappas)[None], (devices, ITERS))
    kappa = jnp.sum(lax.all_to_all(partials, axes, 0, 0, tiled=True), axis=0) * inv_count
    return (deviation, kappa)


def solution(mesh):
    in_specs = (
        P(None, "pb"),
        P("br", "pb", None),
        P("br", None, "pb"),
        P("pb", None),
        P("pb", "br"),
        P("pb", "br"),
    )
    out_specs = (P("pb", "br"), P())
    return jax.shard_map(
        on_device, mesh=mesh, in_specs=in_specs, out_specs=out_specs, check_vma=False
    )
```

```python
from functools import partial

import jax
import jax.numpy as jnp
from jax import lax
from jax.experimental import pallas as pl
from jax.experimental.pallas import tpu as pltpu
from jax.sharding import PartitionSpec as P

ITERS = 2


def split_three(value):
    high = value.astype(jnp.bfloat16)
    rest = value - high.astype(jnp.float32)
    middle = rest.astype(jnp.bfloat16)
    low = (rest - middle.astype(jnp.float32)).astype(jnp.bfloat16)
    return high, middle, low

def spread_kernel(expand_ref, coupling_ref, combined_ref, out_ref):
    @pl.when(pl.program_id(0) == 0)
    def _():
        out_ref[...] = jnp.zeros(out_ref.shape, jnp.float32)

    expand = expand_ref[...]
    rows = None
    for piece in split_three(combined_ref[...]):
        part = jnp.dot(expand, piece, preferred_element_type=jnp.float32)
        rows = part if rows is None else rows + part
    out_ref[...] += jnp.sum(coupling_ref[...] * rows, axis=1, keepdims=True)

def spread_call(coupling_rows, combined, tile=2304):
    rows, cols = coupling_rows.shape
    points = combined.shape[0]
    while cols % tile:
        tile //= 2
    owner = lax.broadcasted_iota(jnp.int32, (rows, points), 0) // (rows // points)
    expand = (owner == lax.broadcasted_iota(jnp.int32, (rows, points), 1)).astype(jnp.bfloat16)
    return pl.pallas_call(
        spread_kernel,
        grid=(cols // tile,),
        in_specs=[
            pl.BlockSpec((rows, points), lambda i: (0, 0)),
            pl.BlockSpec((rows, tile), lambda i: (0, i)),
            pl.BlockSpec((points, tile), lambda i: (0, i)),
        ],
        out_specs=pl.BlockSpec((rows, 1), lambda i: (0, 0)),
        out_shape=jax.ShapeDtypeStruct((rows, 1), jnp.float32),
    )(expand, coupling_rows, combined)

def coupling_kernel(bt_ref, pt_ref, dw_ref, out_ref, acc_ref, *, inv_count):
    pt = pt_ref[...]
    acc_ref[...] = jnp.zeros(acc_ref.shape, jnp.float32)

    def body(n, carry):
        amp = jnp.dot(bt_ref[n], pt, preferred_element_type=jnp.float32)
        acc_ref[...] += amp * amp
        return carry

    lax.fori_loop(0, bt_ref.shape[0], body, 0, unroll=4)
    out_ref[...] = acc_ref[...] * dw_ref[...].astype(jnp.float32) * inv_count


def coupling_call(bt, pt, dw, inv_count, tile=2304):
    comps, rows, m = bt.shape
    cols = pt.shape[1]
    while cols % tile:
        tile //= 2
    return pl.pallas_call(
        partial(coupling_kernel, inv_count=inv_count),
        grid=(cols // tile,),
        in_specs=[
            pl.BlockSpec((comps, rows, m), lambda i: (0, 0, 0)),
            pl.BlockSpec((m, tile), lambda i: (0, i)),
            pl.BlockSpec((rows, tile), lambda i: (0, i)),
        ],
        out_specs=pl.BlockSpec((rows, tile), lambda i: (0, i)),
        out_shape=jax.ShapeDtypeStruct((rows, cols), jnp.float32),
        scratch_shapes=[pltpu.VMEM((rows, tile), jnp.float32)],
    )(bt, pt, dw)


def branch_total(partial_sum):
    own_count = partial_sum.shape[1] // lax.axis_size("br")
    summed = lax.psum(partial_sum, "br")
    return lax.dynamic_slice_in_dim(summed, lax.axis_index("br") * own_count, own_count, 1)


def gather_pb(block, axis):
    count = lax.axis_size("pb")
    copies = jnp.broadcast_to(block[None], (count,) + block.shape)
    got = lax.all_to_all(copies, "pb", 0, 0, tiled=True)
    got = jnp.moveaxis(got, 0, axis)
    shape = list(block.shape)
    shape[axis] *= count
    return got.reshape(shape)


def full_deviation(deviation):
    return gather_pb(deviation, 0)


def on_device(bloch_const, polarization, delta_weight, partner, velocity, capacity):
    local_points = velocity.shape[0]
    own_count = velocity.shape[1]
    all_branches = own_count * lax.axis_size("br")
    total_points = polarization.shape[1] * lax.axis_size("pb")
    inv_count = 1.0 / (total_points * all_branches)
    components = bloch_const.shape[0]
    bt = bloch_const.reshape(components, local_points, all_branches, -1)
    bt = jnp.transpose(bt, (3, 1, 2, 0)).reshape(-1, local_points * all_branches, components)
    pol_all = gather_pb(polarization, 1)
    pt = jnp.transpose(pol_all, (2, 0, 1)).reshape(components, own_count * total_points)
    dw = jnp.transpose(delta_weight.reshape(own_count * total_points, -1))
    coupling_t = coupling_call(bt, pt, dw, inv_count)
    coupling = coupling_t.reshape(local_points, all_branches, own_count * total_points)
    rate_total = branch_total(jnp.sum(coupling, axis=2))
    deviation = velocity / rate_total
    heat_weight = capacity * velocity
    coupling_rows = coupling.reshape(local_points * all_branches, -1)
    targets = lax.broadcasted_iota(jnp.int32, (1, 1, total_points), 2)
    one_hot = (partner[:, :, None] == targets).astype(jnp.bfloat16)
    kappas = []
    for sweep_index in range(ITERS):
        deviation_all = full_deviation(deviation)
        pieces = jnp.concatenate(split_three(deviation_all), axis=1)
        moved = jnp.einsum("qab,bs->qas", one_hot, pieces, preferred_element_type=jnp.float32)
        moved = moved.reshape(local_points, total_points, 3, own_count)
        partner_value = (moved[:, :, 0] + moved[:, :, 1]) + moved[:, :, 2]
        combined = jnp.transpose(deviation_all)[None] + jnp.transpose(partner_value, (0, 2, 1))
        combined = combined.reshape(local_points, -1)
        spread = spread_call(coupling_rows, combined).reshape(local_points, all_branches)
        spread = branch_total(spread)
        deviation = (velocity + 0.5 * spread) / rate_total
        kappas.append(jnp.sum(heat_weight * deviation))
    axes = ("pb", "br")
    devices = lax.axis_size(axes)
    partials = jnp.broadcast_to(jnp.stack(kappas)[None], (devices, ITERS))
    kappa = jnp.sum(lax.all_to_all(partials, axes, 0, 0, tiled=True), axis=0) * inv_count
    return (deviation, kappa)


def solution(mesh):
    in_specs = (
        P(None, "pb"),
        P("br", "pb", None),
        P("br", None, "pb"),
        P("pb", None),
        P("pb", "br"),
        P("pb", "br"),
    )
    out_specs = (P("pb", "br"), P())
    return jax.shard_map(
        on_device, mesh=mesh, in_specs=in_specs, out_specs=out_specs, check_vma=False
    )
```

```python
from functools import partial

import jax
import jax.numpy as jnp
from jax import lax
from jax.experimental import pallas as pl
from jax.experimental.pallas import tpu as pltpu
from jax.sharding import PartitionSpec as P

ITERS = 2


def split_three(value):
    high = value.astype(jnp.bfloat16)
    rest = value - high.astype(jnp.float32)
    middle = rest.astype(jnp.bfloat16)
    low = (rest - middle.astype(jnp.float32)).astype(jnp.bfloat16)
    return high, middle, low

def spread_kernel(expand_ref, coupling_ref, combined_ref, out_ref):
    @pl.when(pl.program_id(0) == 0)
    def _():
        out_ref[...] = jnp.zeros(out_ref.shape, jnp.float32)

    expand = expand_ref[...]
    rows = None
    for piece in split_three(combined_ref[...]):
        part = jnp.dot(expand, piece, preferred_element_type=jnp.float32)
        rows = part if rows is None else rows + part
    out_ref[...] += jnp.sum(coupling_ref[...] * rows, axis=1, keepdims=True)

def spread_call(coupling_rows, combined, tile=2304):
    rows, cols = coupling_rows.shape
    points = combined.shape[0]
    while cols % tile:
        tile //= 2
    owner = lax.broadcasted_iota(jnp.int32, (rows, points), 0) // (rows // points)
    expand = (owner == lax.broadcasted_iota(jnp.int32, (rows, points), 1)).astype(jnp.bfloat16)
    return pl.pallas_call(
        spread_kernel,
        grid=(cols // tile,),
        in_specs=[
            pl.BlockSpec((rows, points), lambda i: (0, 0)),
            pl.BlockSpec((rows, tile), lambda i: (0, i)),
            pl.BlockSpec((points, tile), lambda i: (0, i)),
        ],
        out_specs=pl.BlockSpec((rows, 1), lambda i: (0, 0)),
        out_shape=jax.ShapeDtypeStruct((rows, 1), jnp.float32),
    )(expand, coupling_rows, combined)

def coupling_kernel(bt_ref, pt_ref, dw_ref, out_ref, rate_ref, acc_ref, *, inv_count):
    pt = pt_ref[...]
    acc_ref[...] = jnp.zeros(acc_ref.shape, jnp.float32)

    def body(n, carry):
        amp = jnp.dot(bt_ref[n], pt, preferred_element_type=jnp.float32)
        acc_ref[...] += amp * amp
        return carry

    lax.fori_loop(0, bt_ref.shape[0], body, 0, unroll=9)
    value = acc_ref[...] * dw_ref[...].astype(jnp.float32) * inv_count
    out_ref[...] = value

    @pl.when(pl.program_id(0) == 0)
    def _():
        rate_ref[...] = jnp.zeros(rate_ref.shape, jnp.float32)

    rate_ref[...] += jnp.sum(value, axis=1, keepdims=True)


def coupling_call(bt, pt, dw, inv_count, tile=2304):
    comps, rows, m = bt.shape
    cols = pt.shape[1]
    while cols % tile:
        tile //= 2
    return pl.pallas_call(
        partial(coupling_kernel, inv_count=inv_count),
        grid=(cols // tile,),
        in_specs=[
            pl.BlockSpec((comps, rows, m), lambda i: (0, 0, 0)),
            pl.BlockSpec((m, tile), lambda i: (0, i)),
            pl.BlockSpec((rows, tile), lambda i: (0, i)),
        ],
        out_specs=[
            pl.BlockSpec((rows, tile), lambda i: (0, i)),
            pl.BlockSpec((rows, 1), lambda i: (0, 0)),
        ],
        out_shape=[
            jax.ShapeDtypeStruct((rows, cols), jnp.float32),
            jax.ShapeDtypeStruct((rows, 1), jnp.float32),
        ],
        scratch_shapes=[pltpu.VMEM((rows, tile), jnp.float32)],
    )(bt, pt, dw)


def branch_total(partial_sum):
    own_count = partial_sum.shape[1] // lax.axis_size("br")
    summed = lax.psum(partial_sum, "br")
    return lax.dynamic_slice_in_dim(summed, lax.axis_index("br") * own_count, own_count, 1)


def gather_pb(block, axis):
    count = lax.axis_size("pb")
    copies = jnp.broadcast_to(block[None], (count,) + block.shape)
    got = lax.all_to_all(copies, "pb", 0, 0, tiled=True)
    got = jnp.moveaxis(got, 0, axis)
    shape = list(block.shape)
    shape[axis] *= count
    return got.reshape(shape)


def full_deviation(deviation):
    return gather_pb(deviation, 0)


def on_device(bloch_const, polarization, delta_weight, partner, velocity, capacity):
    local_points = velocity.shape[0]
    own_count = velocity.shape[1]
    all_branches = own_count * lax.axis_size("br")
    total_points = polarization.shape[1] * lax.axis_size("pb")
    inv_count = 1.0 / (total_points * all_branches)
    components = bloch_const.shape[0]
    bt = bloch_const.reshape(components, local_points, all_branches, -1)
    bt = jnp.transpose(bt, (3, 1, 2, 0)).reshape(-1, local_points * all_branches, components)
    pol_all = gather_pb(polarization, 1)
    pt = jnp.transpose(pol_all, (2, 0, 1)).reshape(components, own_count * total_points)
    dw = jnp.transpose(delta_weight.reshape(own_count * total_points, -1))
    coupling_t, rate_partial = coupling_call(bt, pt, dw, inv_count)
    coupling = coupling_t.reshape(local_points, all_branches, own_count * total_points)
    rate_total = branch_total(rate_partial.reshape(local_points, all_branches))
    deviation = velocity / rate_total
    heat_weight = capacity * velocity
    coupling_rows = coupling.reshape(local_points * all_branches, -1)
    targets = lax.broadcasted_iota(jnp.int32, (1, 1, total_points), 2)
    one_hot = (partner[:, :, None] == targets).astype(jnp.bfloat16)
    kappas = []
    for sweep_index in range(ITERS):
        deviation_all = full_deviation(deviation)
        pieces = jnp.concatenate(split_three(deviation_all), axis=1)
        moved = jnp.einsum("qab,bs->qas", one_hot, pieces, preferred_element_type=jnp.float32)
        moved = moved.reshape(local_points, total_points, 3, own_count)
        partner_value = (moved[:, :, 0] + moved[:, :, 1]) + moved[:, :, 2]
        combined = jnp.transpose(deviation_all)[None] + jnp.transpose(partner_value, (0, 2, 1))
        combined = combined.reshape(local_points, -1)
        spread = spread_call(coupling_rows, combined).reshape(local_points, all_branches)
        spread = branch_total(spread)
        deviation = (velocity + 0.5 * spread) / rate_total
        kappas.append(jnp.sum(heat_weight * deviation))
    axes = ("pb", "br")
    devices = lax.axis_size(axes)
    partials = jnp.broadcast_to(jnp.stack(kappas)[None], (devices, ITERS))
    kappa = jnp.sum(lax.all_to_all(partials, axes, 0, 0, tiled=True), axis=0) * inv_count
    return (deviation, kappa)


def solution(mesh):
    in_specs = (
        P(None, "pb"),
        P("br", "pb", None),
        P("br", None, "pb"),
        P("pb", None),
        P("pb", "br"),
        P("pb", "br"),
    )
    out_specs = (P("pb", "br"), P())
    return jax.shard_map(
        on_device, mesh=mesh, in_specs=in_specs, out_specs=out_specs, check_vma=False
    )
```

```python
from functools import partial

import jax
import jax.numpy as jnp
import numpy as np
from jax import lax
from jax.experimental import pallas as pl
from jax.experimental.pallas import tpu as pltpu
from jax.sharding import PartitionSpec as P

ITERS = 2


def split_three(value):
    high = value.astype(jnp.bfloat16)
    rest = value - high.astype(jnp.float32)
    middle = rest.astype(jnp.bfloat16)
    low = (rest - middle.astype(jnp.float32)).astype(jnp.bfloat16)
    return high, middle, low

def spread_kernel(expand_ref, coupling_ref, combined_ref, out_ref):
    @pl.when(pl.program_id(0) == 0)
    def _():
        out_ref[...] = jnp.zeros(out_ref.shape, jnp.float32)

    expand = expand_ref[...]
    rows = None
    for piece in split_three(combined_ref[...]):
        part = jnp.dot(expand, piece, preferred_element_type=jnp.float32)
        rows = part if rows is None else rows + part
    out_ref[...] += jnp.sum(coupling_ref[...] * rows, axis=1, keepdims=True)

def spread_call(coupling_rows, combined, tile=2304):
    rows, cols = coupling_rows.shape
    points = combined.shape[0]
    while cols % tile:
        tile //= 2
    owner = np.arange(rows)[:, None] // (rows // points)
    expand = jnp.asarray(owner == np.arange(points)[None, :], dtype=jnp.bfloat16)
    return pl.pallas_call(
        spread_kernel,
        grid=(cols // tile,),
        in_specs=[
            pl.BlockSpec((rows, points), lambda i: (0, 0)),
            pl.BlockSpec((rows, tile), lambda i: (0, i)),
            pl.BlockSpec((points, tile), lambda i: (0, i)),
        ],
        out_specs=pl.BlockSpec((rows, 1), lambda i: (0, 0)),
        out_shape=jax.ShapeDtypeStruct((rows, 1), jnp.float32),
    )(expand, coupling_rows, combined)

def coupling_kernel(bt_ref, pt_ref, dw_ref, out_ref, rate_ref, acc_ref, *, inv_count):
    pt = pt_ref[...]
    acc_ref[...] = jnp.zeros(acc_ref.shape, jnp.float32)

    def body(n, carry):
        amp = jnp.dot(bt_ref[n], pt, preferred_element_type=jnp.float32)
        acc_ref[...] += amp * amp
        return carry

    lax.fori_loop(0, bt_ref.shape[0], body, 0, unroll=9)
    value = acc_ref[...] * dw_ref[...].astype(jnp.float32) * inv_count
    out_ref[...] = value

    @pl.when(pl.program_id(0) == 0)
    def _():
        rate_ref[...] = jnp.zeros(rate_ref.shape, jnp.float32)

    rate_ref[...] += jnp.sum(value, axis=1, keepdims=True)


def coupling_call(bt, pt, dw, inv_count, tile=2304):
    comps, rows, m = bt.shape
    cols = pt.shape[1]
    while cols % tile:
        tile //= 2
    return pl.pallas_call(
        partial(coupling_kernel, inv_count=inv_count),
        grid=(cols // tile,),
        in_specs=[
            pl.BlockSpec((comps, rows, m), lambda i: (0, 0, 0)),
            pl.BlockSpec((m, tile), lambda i: (0, i)),
            pl.BlockSpec((rows, tile), lambda i: (0, i)),
        ],
        out_specs=[
            pl.BlockSpec((rows, tile), lambda i: (0, i)),
            pl.BlockSpec((rows, 1), lambda i: (0, 0)),
        ],
        out_shape=[
            jax.ShapeDtypeStruct((rows, cols), jnp.float32),
            jax.ShapeDtypeStruct((rows, 1), jnp.float32),
        ],
        scratch_shapes=[pltpu.VMEM((rows, tile), jnp.float32)],
    )(bt, pt, dw)


def branch_total(partial_sum):
    own_count = partial_sum.shape[1] // lax.axis_size("br")
    summed = lax.psum(partial_sum, "br")
    return lax.dynamic_slice_in_dim(summed, lax.axis_index("br") * own_count, own_count, 1)


def gather_pb(block, axis):
    count = lax.axis_size("pb")
    copies = jnp.broadcast_to(block[None], (count,) + block.shape)
    got = lax.all_to_all(copies, "pb", 0, 0, tiled=True)
    got = jnp.moveaxis(got, 0, axis)
    shape = list(block.shape)
    shape[axis] *= count
    return got.reshape(shape)


def full_deviation(deviation):
    return gather_pb(deviation, 0)


def on_device(bloch_const, polarization, delta_weight, partner, velocity, capacity):
    local_points = velocity.shape[0]
    own_count = velocity.shape[1]
    all_branches = own_count * lax.axis_size("br")
    total_points = polarization.shape[1] * lax.axis_size("pb")
    inv_count = 1.0 / (total_points * all_branches)
    components = bloch_const.shape[0]
    bt = bloch_const.reshape(components, local_points, all_branches, -1)
    bt = jnp.transpose(bt, (3, 1, 2, 0)).reshape(-1, local_points * all_branches, components)
    pol_all = gather_pb(polarization, 1)
    pt = jnp.transpose(pol_all, (2, 0, 1)).reshape(components, own_count * total_points)
    dw = jnp.transpose(delta_weight.reshape(own_count * total_points, -1))
    coupling_t, rate_partial = coupling_call(bt, pt, dw, inv_count)
    coupling = coupling_t.reshape(local_points, all_branches, own_count * total_points)
    rate_total = branch_total(rate_partial.reshape(local_points, all_branches))
    deviation = velocity / rate_total
    heat_weight = capacity * velocity
    coupling_rows = coupling.reshape(local_points * all_branches, -1)
    targets = lax.broadcasted_iota(jnp.int32, (1, 1, total_points), 2)
    one_hot = (partner[:, :, None] == targets).astype(jnp.bfloat16)
    kappas = []
    for sweep_index in range(ITERS):
        deviation_all = full_deviation(deviation)
        pieces = jnp.concatenate(split_three(deviation_all), axis=1)
        moved = jnp.einsum("qab,bs->qas", one_hot, pieces, preferred_element_type=jnp.float32)
        moved = moved.reshape(local_points, total_points, 3, own_count)
        partner_value = (moved[:, :, 0] + moved[:, :, 1]) + moved[:, :, 2]
        combined = jnp.transpose(deviation_all)[None] + jnp.transpose(partner_value, (0, 2, 1))
        combined = combined.reshape(local_points, -1)
        spread = spread_call(coupling_rows, combined).reshape(local_points, all_branches)
        spread = branch_total(spread)
        deviation = (velocity + 0.5 * spread) / rate_total
        kappas.append(jnp.sum(heat_weight * deviation))
    axes = ("pb", "br")
    devices = lax.axis_size(axes)
    partials = jnp.broadcast_to(jnp.stack(kappas)[None], (devices, ITERS))
    kappa = jnp.sum(lax.all_to_all(partials, axes, 0, 0, tiled=True), axis=0) * inv_count
    return (deviation, kappa)


def solution(mesh):
    in_specs = (
        P(None, "pb"),
        P("br", "pb", None),
        P("br", None, "pb"),
        P("pb", None),
        P("pb", "br"),
        P("pb", "br"),
    )
    out_specs = (P("pb", "br"), P())
    return jax.shard_map(
        on_device, mesh=mesh, in_specs=in_specs, out_specs=out_specs, check_vma=False
    )
```

```python
from functools import partial

import jax
import jax.numpy as jnp
import numpy as np
from jax import lax
from jax.experimental import pallas as pl
from jax.experimental.pallas import tpu as pltpu
from jax.sharding import PartitionSpec as P

ITERS = 2


def split_three(value):
    high = value.astype(jnp.bfloat16)
    rest = value - high.astype(jnp.float32)
    middle = rest.astype(jnp.bfloat16)
    low = (rest - middle.astype(jnp.float32)).astype(jnp.bfloat16)
    return high, middle, low

def spread_kernel(expand_ref, coupling_ref, combined_ref, out_ref):
    @pl.when(pl.program_id(0) == 0)
    def _():
        out_ref[...] = jnp.zeros(out_ref.shape, jnp.float32)

    rows = jnp.dot(expand_ref[...], combined_ref[...], preferred_element_type=jnp.float32)
    out_ref[...] += jnp.sum(coupling_ref[...] * rows, axis=1, keepdims=True)


def spread_call(coupling_rows, combined, tile=2304):
    rows, cols = coupling_rows.shape
    points = combined.shape[0]
    while cols % tile:
        tile //= 2
    owner = np.arange(rows)[:, None] // (rows // points)
    expand = np.tile(owner == np.arange(points)[None, :], (1, 3))
    expand = jnp.asarray(expand, dtype=jnp.bfloat16)
    combined = jnp.concatenate(split_three(combined), axis=0)
    return pl.pallas_call(
        spread_kernel,
        grid=(cols // tile,),
        in_specs=[
            pl.BlockSpec((rows, 3 * points), lambda i: (0, 0)),
            pl.BlockSpec((rows, tile), lambda i: (0, i)),
            pl.BlockSpec((3 * points, tile), lambda i: (0, i)),
        ],
        out_specs=pl.BlockSpec((rows, 1), lambda i: (0, 0)),
        out_shape=jax.ShapeDtypeStruct((rows, 1), jnp.float32),
    )(expand, coupling_rows, combined)

def coupling_kernel(bt_ref, pt_ref, dw_ref, out_ref, rate_ref, acc_ref, *, inv_count):
    pt = pt_ref[...]
    acc_ref[...] = jnp.zeros(acc_ref.shape, jnp.float32)

    def body(n, carry):
        amp = jnp.dot(bt_ref[n], pt, preferred_element_type=jnp.float32)
        acc_ref[...] += amp * amp
        return carry

    lax.fori_loop(0, bt_ref.shape[0], body, 0, unroll=9)
    value = acc_ref[...] * dw_ref[...].astype(jnp.float32) * inv_count
    out_ref[...] = value

    @pl.when(pl.program_id(0) == 0)
    def _():
        rate_ref[...] = jnp.zeros(rate_ref.shape, jnp.float32)

    rate_ref[...] += jnp.sum(value, axis=1, keepdims=True)


def coupling_call(bt, pt, dw, inv_count, tile=2304):
    comps, rows, m = bt.shape
    cols = pt.shape[1]
    while cols % tile:
        tile //= 2
    return pl.pallas_call(
        partial(coupling_kernel, inv_count=inv_count),
        grid=(cols // tile,),
        in_specs=[
            pl.BlockSpec((comps, rows, m), lambda i: (0, 0, 0)),
            pl.BlockSpec((m, tile), lambda i: (0, i)),
            pl.BlockSpec((rows, tile), lambda i: (0, i)),
        ],
        out_specs=[
            pl.BlockSpec((rows, tile), lambda i: (0, i)),
            pl.BlockSpec((rows, 1), lambda i: (0, 0)),
        ],
        out_shape=[
            jax.ShapeDtypeStruct((rows, cols), jnp.float32),
            jax.ShapeDtypeStruct((rows, 1), jnp.float32),
        ],
        scratch_shapes=[pltpu.VMEM((rows, tile), jnp.float32)],
    )(bt, pt, dw)


def branch_total(partial_sum):
    own_count = partial_sum.shape[1] // lax.axis_size("br")
    summed = lax.psum(partial_sum, "br")
    return lax.dynamic_slice_in_dim(summed, lax.axis_index("br") * own_count, own_count, 1)


def gather_pb(block, axis):
    count = lax.axis_size("pb")
    copies = jnp.broadcast_to(block[None], (count,) + block.shape)
    got = lax.all_to_all(copies, "pb", 0, 0, tiled=True)
    got = jnp.moveaxis(got, 0, axis)
    shape = list(block.shape)
    shape[axis] *= count
    return got.reshape(shape)


def full_deviation(deviation):
    return gather_pb(deviation, 0)


def on_device(bloch_const, polarization, delta_weight, partner, velocity, capacity):
    local_points = velocity.shape[0]
    own_count = velocity.shape[1]
    all_branches = own_count * lax.axis_size("br")
    total_points = polarization.shape[1] * lax.axis_size("pb")
    inv_count = 1.0 / (total_points * all_branches)
    components = bloch_const.shape[0]
    bt = bloch_const.reshape(components, local_points, all_branches, -1)
    bt = jnp.transpose(bt, (3, 1, 2, 0)).reshape(-1, local_points * all_branches, components)
    pol_all = gather_pb(polarization, 1)
    pt = jnp.transpose(pol_all, (2, 0, 1)).reshape(components, own_count * total_points)
    dw = jnp.transpose(delta_weight.reshape(own_count * total_points, -1))
    coupling_t, rate_partial = coupling_call(bt, pt, dw, inv_count)
    coupling = coupling_t.reshape(local_points, all_branches, own_count * total_points)
    rate_total = branch_total(rate_partial.reshape(local_points, all_branches))
    deviation = velocity / rate_total
    heat_weight = capacity * velocity
    coupling_rows = coupling.reshape(local_points * all_branches, -1)
    targets = lax.broadcasted_iota(jnp.int32, (1, 1, total_points), 2)
    one_hot = (partner[:, :, None] == targets).astype(jnp.bfloat16)
    kappas = []
    for sweep_index in range(ITERS):
        deviation_all = full_deviation(deviation)
        pieces = jnp.concatenate(split_three(deviation_all), axis=1)
        moved = jnp.einsum("qab,bs->qas", one_hot, pieces, preferred_element_type=jnp.float32)
        moved = moved.reshape(local_points, total_points, 3, own_count)
        partner_value = (moved[:, :, 0] + moved[:, :, 1]) + moved[:, :, 2]
        combined = jnp.transpose(deviation_all)[None] + jnp.transpose(partner_value, (0, 2, 1))
        combined = combined.reshape(local_points, -1)
        spread = spread_call(coupling_rows, combined).reshape(local_points, all_branches)
        spread = branch_total(spread)
        deviation = (velocity + 0.5 * spread) / rate_total
        kappas.append(jnp.sum(heat_weight * deviation))
    axes = ("pb", "br")
    devices = lax.axis_size(axes)
    partials = jnp.broadcast_to(jnp.stack(kappas)[None], (devices, ITERS))
    kappa = jnp.sum(lax.all_to_all(partials, axes, 0, 0, tiled=True), axis=0) * inv_count
    return (deviation, kappa)


def solution(mesh):
    in_specs = (
        P(None, "pb"),
        P("br", "pb", None),
        P("br", None, "pb"),
        P("pb", None),
        P("pb", "br"),
        P("pb", "br"),
    )
    out_specs = (P("pb", "br"), P())
    return jax.shard_map(
        on_device, mesh=mesh, in_specs=in_specs, out_specs=out_specs, check_vma=False
    )
```
